256 devices in a mesh: row: 16 (over x, z_lo), col: 16 (over z_hi, y, core).
Axes of the slice: x: 4, y: 4, z: 8 (z_hi: 2, z_lo: 4; z = z_hi * 4 + z_lo), core: 2. Of those that a mesh axis runs over, the one named last changes fastest.
Arguments:
- acts: bfloat16 [2048, 5120], P('col', 'row'), may hold values from -60 to 60
- out_grads: bfloat16 [2048, 13824], P('row', 'col'), may hold values from -0.06187184 to 0.06187184
- momentum: float32 [5120, 13824], P('row', 'col'), may hold values from -200 to 200
- weight: float32 [5120, 13824], P('row', 'col'), may hold values from -0.078125 to 0.078125
Outputs:
- momentum_new: float32 [5120, 13824], P('row', 'col')
- update: bfloat16 [5120, 13824], P('row', 'col')
- weight_new: float32 [5120, 13824], P('row', 'col')
The draws below stay inside these ranges and needn't reach their ends.
All inputs are finite; a program needn't handle non-finite values.
Results may differ from the reference program's by a relative error of at most 0.014.
Values may be sent and summed in bfloat16 or wider, within the bound.
A program may use at most 64 MiB of HBM per device.

```python
import math
import jax
import jax.numpy as jnp
from jax import lax

D = 5120
F = 13824
TOKENS = 2048
N_COL = 16


def draw_acts(key, part):
    key_values = jax.random.fold_in(key, 11)
    key_jitter = jax.random.fold_in(key, 12)
    values = jnp.clip(jax.random.normal(key_values, (TOKENS, D), jnp.float32), -6.0, 6.0)
    jitter = jax.random.uniform(key_jitter, (D,), jnp.float32)
    position = jnp.arange(D, dtype=jnp.float32) / D
    scales = jnp.power(10.0, 0.5 * position + 0.5 * jitter)
    return (values * scales[None, :]).astype(jnp.bfloat16)


def draw_out_grads(key, part):
    key_values = jax.random.fold_in(key, 21)
    key_jitter = jax.random.fold_in(key, 22)
    values = jnp.clip(jax.random.normal(key_values, (TOKENS, F), jnp.float32), -4.0, 4.0)
    jitter = jax.random.uniform(key_jitter, (F,), jnp.float32)
    position = jnp.arange(F, dtype=jnp.float32) / F
    scales = jnp.power(10.0, 0.5 * position + 0.5 * jitter)
    return (values * scales[None, :] * (0.07 / jnp.sqrt(jnp.float32(TOKENS)))).astype(jnp.bfloat16)


def draw_momentum(key, part):
    key_left = jax.random.fold_in(key, 31)
    key_right = jax.random.fold_in(key, 32)
    key_noise = jax.random.fold_in(key, 33)
    key_rowjit = jax.random.fold_in(key, 34)
    key_coljit = jax.random.fold_in(key, 35)
    row_position = jnp.arange(D, dtype=jnp.float32) / D
    col_position = jnp.arange(F, dtype=jnp.float32) / F
    row_jitter = jax.random.uniform(key_rowjit, (D,), jnp.float32)
    col_jitter = jax.random.uniform(key_coljit, (F,), jnp.float32)
    row_scale = jnp.power(10.0, 0.5 * row_position + 0.5 * row_jitter)
    col_scale = jnp.power(10.0, 0.5 * col_position + 0.5 * col_jitter) / 4.6
    left = jnp.clip(jax.random.normal(key_left, (D,), jnp.float32), -4.0, 4.0)
    right = jnp.clip(jax.random.normal(key_right, (F,), jnp.float32), -4.0, 4.0)
    noise = 2.0 * jnp.clip(jax.random.normal(key_noise, (D, F), jnp.float32), -4.0, 4.0)
    left = left * jnp.power(10.0, jnp.cos(4.0 * jnp.pi * row_position)) / 4.6
    planted = 0.65 * left[:, None] * right[None, :]
    return (planted + noise * row_scale[:, None] * col_scale[None, :]).astype(jnp.float32)


def block_scale(key, extent, shards, smallest, largest):
    gain = 1.0
    for dim, shards_of in shards:
        steps = jax.random.uniform(jax.random.fold_in(jax.random.fold_in(key, 6), dim), (shards_of,), jnp.float32, smallest / len(shards), largest / len(shards))
        gain = gain * jnp.repeat(jnp.exp(steps), extent[dim] // shards_of).reshape((-1,) + (1,) * (len(extent) - 1 - dim))
    return gain


def normal_values(key, shape, deviation, bound, shards=(), held_as=jnp.bfloat16):
    values = jax.random.normal(key, shape, jnp.float32) * deviation
    if len(shards) > 0:
        values = block_scale(key, shape, shards, -0.22, 0.18) * values
    return jnp.clip(values, min=-bound, max=bound).astype(held_as)


def setup_inputs(seed: int = 0) -> dict:
    key_of = jax.random.split(jax.random.key(seed), 5)
    acts = draw_acts(jax.random.fold_in(key_of[4], 71), 0)
    out_grads = draw_out_grads(jax.random.fold_in(key_of[4], 71), 0)
    momentum = draw_momentum(jax.random.fold_in(key_of[4], 71), 0)
    weight = normal_values(key_of[3], (D, F), D ** -0.5, 0.078125, ((0, 16), (1, 16)), jnp.float32)
    return dict(acts=acts, out_grads=out_grads, momentum=momentum, weight=weight)


def reference(acts, out_grads, momentum, weight):
    gradient = jnp.dot(acts.T, out_grads, preferred_element_type=jnp.float32)
    momentum_new = 0.95 * momentum + gradient
    blended = gradient + 0.95 * momentum_new
    rounded = blended.astype(jnp.bfloat16)
    block_width = F // N_COL
    gram_sum = jnp.zeros((D, D), jnp.float32)
    for column_block in range(N_COL):
        pieces = rounded[:, column_block * block_width:(column_block + 1) * block_width]
        partial_value = jnp.dot(pieces, pieces.T, preferred_element_type=jnp.float32).astype(jnp.bfloat16)
        partial_value = lax.optimization_barrier(partial_value)
        gram_sum = gram_sum + partial_value.astype(jnp.float32)
    gram = gram_sum.astype(jnp.bfloat16)
    gram_square = jnp.dot(gram, gram, preferred_element_type=jnp.float32)
    schatten = jnp.sqrt(jnp.sum(gram_square * gram_square) + 1e-06)
    square_root = jnp.sqrt(schatten)
    fourth_root = jnp.sqrt(square_root)
    poly = (-4.775 * gram.astype(jnp.float32) / square_root + 2.0315 * gram_square / schatten).astype(jnp.bfloat16)
    product = jnp.dot(poly, rounded, preferred_element_type=jnp.float32)
    orthogonal = (3.4445 * rounded.astype(jnp.float32) + product) / fourth_root
    factor = math.sqrt(D)
    update = (factor * orthogonal).astype(jnp.bfloat16)
    weight_new = 0.998 * weight - 0.02 * factor * orthogonal
    return (momentum_new, update, weight_new)
```

```python
import math

import jax
import jax.numpy as jnp
from jax import lax
from jax.experimental import pallas as pl
from jax.experimental.pallas import tpu as pltpu
from jax.sharding import PartitionSpec as P

D = 5120
MESH = pl.DeviceIdType.MESH
F32 = jnp.float32
BF16 = jnp.bfloat16
N_SEM = 480


def dot_nn(a, b):
    return jnp.dot(a, b, preferred_element_type=F32)


def dot_nt(a, b):
    return lax.dot_general(a, b, (((1,), (1,)), ((), ())), preferred_element_type=F32)


class Comm:
    def __init__(self, sems):
        self.sems = sems
        self.used = 0
        self.pending = []
        self.r = lax.axis_index("row")
        self.c = lax.axis_index("col")
        r, c = self.r, self.c
        self.x, self.zl = r // 4, r % 4
        self.zh, self.y, self.co = c // 8, (c // 2) % 4, c % 2
        self.s = self.zl // 2
        self.zm = self.zl + self.s * (3 - 2 * self.zl)
        self.inner = self.zm == 1

    def sem(self, n=1):
        base = self.used
        self.used += n
        assert self.used <= N_SEM
        return base

    def row_dev(self, xo, zo):
        return (((self.x + xo + 4) % 4) * 4 + self.zl + zo * (1 - 2 * self.s), self.c)

    def y_dev(self, yo):
        return (self.r, self.zh * 8 + ((self.y + yo) % 4) * 2 + self.co)

    def zh_dev(self):
        return (self.r, (1 - self.zh) * 8 + self.y * 2 + self.co)

    def core_dev(self):
        return (self.r, self.zh * 8 + self.y * 2 + 1 - self.co)

    def zs(self, j):
        v = (self.zm, 1 - self.zm, 2, 3)[j]
        return v + self.s * (3 - 2 * v)

    def send(self, src, dst, ssem, rsem, to, cond=None):
        copy = pltpu.make_async_remote_copy(
            src_ref=src, dst_ref=dst, send_sem=self.sems.at[ssem], recv_sem=self.sems.at[rsem],
            device_id=to, device_id_type=MESH,
        )
        if cond is None:
            copy.start()
        else:
            pl.when(cond)(copy.start)
        self.pending.append((copy, cond))

    def recv(self, dst, rsem, cond=None):
        copy = pltpu.make_async_remote_copy(
            src_ref=dst, dst_ref=dst, send_sem=self.sems.at[rsem], recv_sem=self.sems.at[rsem],
            device_id=self.core_dev(), device_id_type=MESH,
        )
        if cond is None:
            copy.wait_recv()
        else:
            pl.when(cond)(copy.wait_recv)

    def drain(self):
        for copy, cond in self.pending:
            if cond is None:
                copy.wait_send()
            else:
                pl.when(cond)(copy.wait_send)
        self.pending = []


def row_gather(cm, view, half, own):
    rz, rp, rm, h0, h1 = (cm.sem(4) for _ in range(5))
    sz, sz2, sp, sm, t0, t1 = (cm.sem(4) for _ in range(6))

    def block(xo, j):
        return ((cm.x + xo + 4) % 4) * 4 + cm.zs(j)

    def out_x(j):
        k, zs = block(0, j), cm.zs(j)
        src = own if j == 0 else view(k)
        cm.send(src, view(k), sp + j, rp + zs, cm.row_dev(1, 0))
        cm.send(src, view(k), sm + j, rm + zs, cm.row_dev(-1, 0))

    def on_x(j):
        k, zs = block(-1, j), cm.zs(j)
        cm.recv(view(k), rp + zs)
        cm.send(half(k, 0), half(k, 0), t0 + j, h0 + zs, cm.row_dev(1, 0))
        k = block(1, j)
        cm.recv(view(k), rm + zs)
        cm.send(half(k, 1), half(k, 1), t1 + j, h1 + zs, cm.row_dev(-1, 0))

    k = block(0, 0)
    cm.send(own, view(k), sz, rz + cm.zl, cm.row_dev(0, 1))
    cm.send(own, view(k), sz2, rz + cm.zl, cm.row_dev(0, -1), cm.inner)
    out_x(0)
    yield (0, 0)
    for j in range(1, 4):
        k, zs = block(0, j), cm.zs(j)
        cm.recv(view(k), rz + zs)
        cm.send(view(k), view(k), sz + j, rz + zs, cm.row_dev(0, 1 if j == 1 else -1), cm.inner)
        out_x(j)
        yield (0, j)
        on_x(j - 1)
        yield (1, j - 1)
        yield (-1, j - 1)
    on_x(3)
    yield (1, 3)
    yield (-1, 3)
    for j in range(4):
        k, zs = block(2, j), cm.zs(j)
        cm.recv(half(k, 0), h0 + zs)
        cm.recv(half(k, 1), h1 + zs)
        yield (2, j)


def col_gather(cm, view, own):
    rzh, ry, rc = cm.sem(), cm.sem(6), cm.sem(8)
    szh, sy, sc = cm.sem(), cm.sem(6), cm.sem(8)

    def idx(zh, yo):
        return zh * 8 + ((cm.y + yo) % 4) * 2 + cm.co

    me = idx(cm.zh, 0)
    cm.send(own, view(me), szh, rzh, cm.zh_dev())
    for i, yo in enumerate((1, 3, 2)):
        cm.send(own, view(me), sy + i, ry + i, cm.y_dev(yo))
    cm.send(own, view(me), sc, rc, cm.core_dev())
    yield 0
    k = idx(1 - cm.zh, 0)
    cm.recv(view(k), rzh)
    for i, yo in enumerate((1, 3, 2)):
        cm.send(view(k), view(k), sy + 3 + i, ry + 3 + i, cm.y_dev(yo))
    cm.send(view(k), view(k), sc + 4, rc + 4, cm.core_dev())
    yield 1
    for zo in (0, 1):
        for i, yo in enumerate((1, 3, 2)):
            k = idx(cm.zh + zo * (1 - 2 * cm.zh), -yo + 4)
            cm.recv(view(k), ry + 3 * zo + i)
            cm.send(view(k), view(k), sc + 4 * zo + 1 + i, rc + 4 * zo + 1 + i, cm.core_dev())
        yield 2 + zo
    for zo in (0, 1):
        for i, yo in enumerate((0, 1, 3, 2)):
            k = idx(cm.zh + zo * (1 - 2 * cm.zh), -yo + 4) + 1 - 2 * cm.co
            cm.recv(view(k), rc + 4 * zo + i)
        yield 4 + zo


def kernel(acts_ref, og_ref, m_hbm, w_hbm, mnew_ref, upd_ref, wnew_ref,
           actb, ogb, rb, pb, rcb, csb, ryb, rzb, gb, hb, sb, acc1, acc2, gsq, mv, wv, ss1, ss2,
           sems, lsem):
    cm = Comm(sems)
    r, c = cm.r, cm.c
    tr, tc = mnew_ref.shape
    tt = og_ref.shape[0]

    load_m = pltpu.make_async_copy(m_hbm, mv, lsem.at[0])
    load_w = pltpu.make_async_copy(w_hbm, wv, lsem.at[1])
    load_m.start()
    load_w.start()

    barrier = pltpu.get_barrier_semaphore()
    for i in range(1, 16):
        pl.semaphore_signal(barrier, inc=1, device_id=((r + i) % 16, c), device_id_type=MESH)
        pl.semaphore_signal(barrier, inc=1, device_id=(r, (c + i) % 16), device_id_type=MESH)
    pl.semaphore_wait(barrier, 30)

    def og_view(k):
        return ogb.at[pl.ds(pl.multiple_of(k * tt, tt), tt)]

    def og_half(k, h):
        return ogb.at[pl.ds(pl.multiple_of(k * tt + h * (tt // 2), tt // 2), tt // 2)]

    def act_view(k):
        return actb.at[:, pl.ds(pl.multiple_of(k * tt, tt), tt)]

    gc = col_gather(cm, act_view, acts_ref)
    gr = row_gather(cm, og_view, og_half, og_ref)
    next(gr)
    next(gc)
    og_view(r)[...] = og_ref[...]
    act_view(c)[...] = acts_ref[...]
    for event in gr:
        if event in ((0, 1), (0, 2), (0, 3), (1, 3)):
            next(gc)
    for _ in gc:
        pass
    acc1[...] = jnp.zeros_like(acc1)

    @pl.loop(0, 2048 // 256)
    def _(t):
        at = pl.multiple_of(t * 256, 256)
        acc1[...] += dot_nn(actb[:, pl.ds(at, 256)], ogb[pl.ds(at, 256), :])

    load_m.wait()
    gradient = acc1[...]
    m_new = 0.95 * mv[...] + gradient
    mnew_ref[...] = m_new
    rb[r] = (gradient + 0.95 * m_new).astype(BF16)

    rc1, sc1 = cm.sem(8), cm.sem(8)
    rcy, scy = cm.sem(6), cm.sem(8)
    rzx, szx = cm.sem(), cm.sem()
    done = []

    def pair_of(xo, far):
        near_pair = cm.s
        return ((cm.x + xo + 4) % 4) * 2 + near_pair + far * (1 - 2 * near_pair)

    def core_send(n, p):
        cm.send(pb.at[2 * p + 1 - cm.co], rcb.at[p], sc1 + n, rc1 + p, cm.core_dev())

    def core_done(n, p):
        cm.recv(rcb.at[p], rc1 + p)
        csb[p] = (pb[2 * p + cm.co].astype(F32) + rcb[p].astype(F32)).astype(BF16)
        zh, y = p // 4, p % 4
        slot = (cm.y + 3 - y + 4) % 4
        far = y != cm.y
        cm.send(csb.at[p], ryb.at[zh * 3 + slot % 3], scy + n, rcy + zh * 3 + slot % 3,
                (r, cm.zh * 8 + y * 2 + cm.co), far)

    def gram_block(k):
        pb[k] = dot_nt(rb[r], rb[k]).astype(BF16)

    pairs = {}
    order = []
    for xo, j in row_gather(cm, lambda k: rb.at[k], lambda k, h: rb.at[k, pl.ds(h * (tr // 2), tr // 2)], rb.at[r]):
        gram_block(((cm.x + xo + 4) % 4) * 4 + cm.zs(j))
        key = (xo, j // 2)
        pairs[key] = pairs.get(key, 0) + 1
        if pairs[key] == 2:
            n = len(order)
            p = pair_of(*key)
            core_send(n, p)
            if order:
                core_done(n - 1, order[-1])
            order.append(p)
    core_done(7, order[-1])

    def y_sum(zh):
        for i in range(3):
            cm.recv(ryb.at[zh * 3 + i], rcy + zh * 3 + i)
        return (csb[zh * 4 + cm.y].astype(F32) + ryb[zh * 3].astype(F32)
                + ryb[zh * 3 + 1].astype(F32) + ryb[zh * 3 + 2].astype(F32))

    far_sum = rcb.at[0]
    far_sum[...] = y_sum(1 - cm.zh).astype(BF16)
    cm.send(far_sum, rzb, szx, rzx, cm.zh_dev())
    near_sum = y_sum(cm.zh)
    cm.recv(rzb, rzx)
    tile = (near_sum + rzb[...].astype(F32)).astype(BF16)
    gb[c] = tile
    hb[r] = tile

    gc = col_gather(cm, lambda k: gb.at[k], gb.at[c])
    gr = row_gather(cm, lambda k: hb.at[k], lambda k, h: hb.at[k, pl.ds(h * (tr // 2), tr // 2)], hb.at[r])
    next(gr)
    next(gc)
    for event in gr:
        if event in ((0, 1), (0, 2), (0, 3), (1, 3), (-1, 3)):
            next(gc)
    for _ in gc:
        pass
    gsq[...] = jnp.zeros_like(gsq)

    @pl.loop(0, 16)
    def _(k):
        gsq[...] += dot_nn(gb[k], hb[k])

    sb[c] = gsq[...].astype(BF16)

    gc = col_gather(cm, lambda k: sb.at[k], sb.at[c])
    next(gc)
    squares = jnp.sum(gsq[...] * gsq[...], axis=0, keepdims=True)
    ss1[r] = jnp.broadcast_to(jnp.sum(squares, axis=1, keepdims=True), ss1.shape[1:])
    r1, s1, r2, s2 = cm.sem(16), cm.sem(16), cm.sem(16), cm.sem(16)
    for i in range(1, 16):
        cm.send(ss1.at[r], ss1.at[r], s1 + i, r1 + i, ((r + i) % 16, c))
    acc1[...] = jnp.zeros_like(acc1)
    acc2[...] = jnp.zeros_like(acc2)

    def gram_times(lo, hi):
        @pl.loop(lo, hi)
        def _(k):
            acc1[...] += dot_nn(gb[k], rb[k])

    def square_times(zh, co):
        @pl.loop(0, 4)
        def _(y):
            k = zh * 8 + y * 2 + co
            acc2[...] += dot_nn(sb[k], rb[k])

    gram_times(0, 6)
    for i in range(1, 16):
        cm.recv(ss1.at[(r - i + 16) % 16], r1 + i)
    ss2[c] = jnp.sum(ss1[...], axis=0)
    for i in range(1, 16):
        cm.send(ss2.at[c], ss2.at[c], s2 + i, r2 + i, (r, (c + i) % 16))
    next(gc)
    gram_times(6, 11)
    next(gc)
    gram_times(11, 16)
    square_times(cm.zh, cm.co)
    next(gc)
    square_times(1 - cm.zh, cm.co)
    next(gc)
    square_times(cm.zh, 1 - cm.co)
    next(gc)
    square_times(1 - cm.zh, 1 - cm.co)
    for _ in gc:
        pass
    for i in range(1, 16):
        cm.recv(ss2.at[(c - i + 16) % 16], r2 + i)
    total = jnp.sum(ss2[...], axis=0)[0:1, 0:1]
    schatten = jnp.sqrt(total + 1e-06)
    square_root = jnp.sqrt(schatten)
    fourth_root = jnp.sqrt(square_root)
    load_w.wait()
    product = -4.775 * acc1[...] / square_root + 2.0315 * acc2[...] / schatten
    orthogonal = (3.4445 * rb[r].astype(F32) + product) / fourth_root
    factor = math.sqrt(D)
    upd_ref[...] = (factor * orthogonal).astype(BF16)
    wnew_ref[...] = 0.998 * wv[...] - 0.02 * factor * orthogonal
    cm.drain()


def body(acts, out_grads, momentum, weight):
    tr, tc = momentum.shape
    tt = out_grads.shape[0]
    vmem = pl.BlockSpec(memory_space=pltpu.VMEM)
    hbm = pl.BlockSpec(memory_space=pl.ANY)
    block = (tr, tr)
    return pl.pallas_call(
        kernel,
        name="muon_step",
        out_shape=(
            jax.ShapeDtypeStruct((tr, tc), F32),
            jax.ShapeDtypeStruct((tr, tc), BF16),
            jax.ShapeDtypeStruct((tr, tc), F32),
        ),
        in_specs=[vmem, vmem, hbm, hbm],
        out_specs=[vmem, vmem, vmem],
        scratch_shapes=[
            pltpu.VMEM((tr, 16 * tt), BF16),
            pltpu.VMEM((16 * tt, tc), BF16),
            pltpu.VMEM((16, tr, tc), BF16),
            pltpu.VMEM((16,) + block, BF16),
            pltpu.VMEM((8,) + block, BF16),
            pltpu.VMEM((8,) + block, BF16),
            pltpu.VMEM((6,) + block, BF16),
            pltpu.VMEM(block, BF16),
            pltpu.VMEM((16,) + block, BF16),
            pltpu.VMEM((16,) + block, BF16),
            pltpu.VMEM((16,) + block, BF16),
            pltpu.VMEM((tr, tc), F32),
            pltpu.VMEM((tr, tc), F32),
            pltpu.VMEM(block, F32),
            pltpu.VMEM((tr, tc), F32),
            pltpu.VMEM((tr, tc), F32),
            pltpu.VMEM((16, 8, 128), F32),
            pltpu.VMEM((16, 8, 128), F32),
            pltpu.SemaphoreType.DMA((N_SEM,)),
            pltpu.SemaphoreType.DMA((2,)),
        ],
        compiler_params=pltpu.CompilerParams(
            collective_id=0, has_side_effects=True, vmem_limit_bytes=67043328
        ),
    )(acts.T, out_grads, momentum, weight)


def solution(mesh):
    in_specs = (P("col", "row"), P("row", "col"), P("row", "col"), P("row", "col"))
    out_specs = (P("row", "col"), P("row", "col"), P("row", "col"))
    return jax.shard_map(body, mesh=mesh, in_specs=in_specs, out_specs=out_specs, check_vma=False)
```

```python
import math

import jax
import jax.numpy as jnp
from jax import lax
from jax.experimental import pallas as pl
from jax.experimental.pallas import tpu as pltpu
from jax.sharding import PartitionSpec as P

D = 5120
MESH = pl.DeviceIdType.MESH
F32 = jnp.float32
BF16 = jnp.bfloat16
N_SEM = 200
PAIR = 640
WIDE = (384, 256)


def dot_nn(a, b):
    return jnp.dot(a, b, preferred_element_type=F32)


def dot_nt(a, b):
    return lax.dot_general(a, b, (((1,), (1,)), ((), ())), preferred_element_type=F32)


def ds(start, size, unit):
    return pl.ds(pl.multiple_of(start, unit), size)


class Comm:
    def __init__(self, sems):
        self.sems = sems
        self.used = 0
        self.drains = []
        self.r = lax.axis_index("row")
        self.c = lax.axis_index("col")
        r, c = self.r, self.c
        self.x, self.zl = r // 4, r % 4
        self.zh, self.y, self.co = c // 8, (c // 2) % 4, c % 2
        self.q = c // 2
        self.s = self.zl // 2
        self.zm = self.zl + self.s * (3 - 2 * self.zl)
        self.inner = self.zm == 1

    def sem(self, n=1):
        base = self.used
        self.used += n
        assert self.used <= N_SEM
        return base

    def row_dev(self, xo, zo):
        return (((self.x + xo + 4) % 4) * 4 + self.zl + zo * (1 - 2 * self.s), self.c)

    def y_dev(self, yo):
        return (self.r, self.zh * 8 + ((self.y + yo) % 4) * 2 + self.co)

    def zh_dev(self):
        return (self.r, (1 - self.zh) * 8 + self.y * 2 + self.co)

    def core_dev(self):
        return (self.r, self.q * 2 + 1 - self.co)

    def zs(self, j):
        v = (self.zm, 1 - self.zm, 2, 3)[j]
        return v + self.s * (3 - 2 * v)

    def row_block(self, xo, j):
        return ((self.x + xo + 4) % 4) * 4 + self.zs(j)

    def row_pair(self, xo, far):
        return ((self.x + xo + 4) % 4) * 2 + self.s + far * (1 - 2 * self.s)

    def copy(self, src, dst, ssem, rsem, to):
        return pltpu.make_async_remote_copy(
            src_ref=src, dst_ref=dst, send_sem=self.sems.at[ssem], recv_sem=self.sems.at[rsem],
            device_id=to, device_id_type=MESH,
        )

    def send(self, ref, ssem, rsem, to):
        self.copy(ref, ref, ssem, rsem, to).start()

    def recv(self, ref, rsem):
        self.copy(ref, ref, rsem, rsem, self.core_dev()).wait_recv()

    def drain_later(self, ref, ssem, cond=None):
        self.drains.append((ref, ssem, cond))

    def drain(self):
        for ref, ssem, cond in self.drains:
            def wait():
                self.copy(ref, ref, ssem, ssem, self.core_dev()).wait_send()
            if cond is None:
                wait()
            else:
                pl.when(cond)(wait)

    def cores(self, split):
        return ((0, self.co == 0), (1, self.co == 1)) if split else ((self.co, None),)


def guarded(cond):
    return pl.when(cond) if cond is not None else lambda f: f()


def row_gather(cm, view, span, na, nb, split=False):
    az, ap, am, ah = (cm.sem(4) for _ in range(4))
    bp, bm, bh, bz = cm.sem(), cm.sem(), cm.sem(), cm.sem(16)
    s_all, s_in = cm.sem(), cm.sem()
    ha, hb = na // 2, nb // 2
    sel = ((1, 0), (-1, 0))
    xi = {0: 0, 1: 1, -1: 2, 2: 3}

    def a(k, co, lo=0, n=na):
        return view(k, lo, n, co)

    def b(k, co, lo=0, n=nb):
        return view(k, na + lo, n, co)

    def each(f):
        for co, cond in cm.cores(split):
            guarded(cond)(lambda: f(co))

    def inner(f):
        pl.when(cm.inner)(f)

    def a_out(j):
        k, zs = cm.row_block(0, j), cm.zs(j)

        def f(co):
            cm.send(a(k, co), s_all, ap + zs, cm.row_dev(1, 0))
            cm.send(a(k, co), s_all, am + zs, cm.row_dev(-1, 0))
        each(f)

    def a_chain(j):
        k, zs = cm.row_block(0, j), cm.zs(j)

        def f(co):
            cm.recv(a(k, co), az + zs)
            inner(lambda: cm.send(a(k, co), s_in, az + zs, cm.row_dev(0, 1 if j == 1 else -1)))
        each(f)
        a_out(j)

    def a_ring(j):
        zs = cm.zs(j)

        def f(co):
            k = cm.row_block(-1, j)
            cm.recv(a(k, co), ap + zs)
            cm.send(a(k, co, 0, ha), s_all, ah + zs, cm.row_dev(1, 0))
            k = cm.row_block(1, j)
            cm.recv(a(k, co), am + zs)
            cm.send(a(k, co, ha, ha), s_all, ah + zs, cm.row_dev(-1, 0))
        each(f)

    def a_last(j):
        each(lambda co: cm.recv(a(cm.row_block(2, j), co), ah + cm.zs(j)))

    def b_out(xo):
        k = cm.row_block(xo, 0)

        def f(co):
            cm.send(b(k, co), s_all, bz + 4 * xi[xo] + cm.zl, cm.row_dev(0, 1))
            inner(lambda: cm.send(b(k, co), s_in, bz + 4 * xi[xo] + cm.zl, cm.row_dev(0, -1)))
        each(f)

    def b_chain(xo, j):
        k, sem = cm.row_block(xo, j), bz + 4 * xi[xo] + cm.zs(j)

        def f(co):
            cm.recv(b(k, co), sem)
            inner(lambda: cm.send(b(k, co), s_in, sem, cm.row_dev(0, 1 if j == 1 else -1)))
        each(f)

    def start(co):
        k = cm.r
        cm.send(b(k, co), s_all, bp, cm.row_dev(1, 0))
        cm.send(b(k, co), s_all, bm, cm.row_dev(-1, 0))
        cm.send(a(k, co), s_all, az + cm.zl, cm.row_dev(0, 1))
        inner(lambda: cm.send(a(k, co), s_in, az + cm.zl, cm.row_dev(0, -1)))

    def b_ring(co):
        k = cm.row_block(-1, 0)
        cm.recv(b(k, co), bp)
        cm.send(b(k, co, 0, hb), s_all, bh, cm.row_dev(1, 0))
        k = cm.row_block(1, 0)
        cm.recv(b(k, co), bm)
        cm.send(b(k, co, hb, hb), s_all, bh, cm.row_dev(-1, 0))

    each(start)
    a_out(0)
    b_out(0)
    yield "start"
    each(b_ring)
    b_out(1)
    b_out(-1)
    a_chain(1)
    b_chain(0, 1)
    yield (0, 0)
    a_ring(0)
    each(lambda co: cm.recv(b(cm.row_block(2, 0), co), bh))
    b_out(2)
    a_chain(2)
    b_chain(1, 1)
    b_chain(-1, 1)
    b_chain(0, 2)
    a_ring(1)
    yield (1, 0)
    yield (-1, 0)
    a_chain(3)
    b_chain(2, 1)
    b_chain(0, 3)
    yield (0, 1)
    b_chain(1, 2)
    b_chain(-1, 2)
    a_ring(2)
    b_chain(2, 2)
    a_ring(3)
    b_chain(1, 3)
    b_chain(-1, 3)
    yield (1, 1)
    yield (-1, 1)
    a_last(0)
    a_last(1)
    yield (2, 0)
    b_chain(2, 3)
    a_last(2)
    a_last(3)
    yield (2, 1)
    for co, cond in cm.cores(split):
        cm.drain_later(span(13 * na + 7 * nb, co), s_all, cond)
        both = cm.inner if cond is None else jnp.logical_and(cm.inner, cond)
        cm.drain_later(span(4 * na + 16 * nb, co), s_in, both)


def col_gather(cm, view, span, rows, split=False):
    rz, rp, rm, rh, rc = cm.sem(), cm.sem(2), cm.sem(2), cm.sem(2), cm.sem(8)
    s_all, s_core = cm.sem(), cm.sem()
    half = rows // 2

    def chip(zo, yo):
        return (cm.zh + zo * (1 - 2 * cm.zh)) * 4 + (cm.y + yo + 4) % 4

    def each(f):
        for co, cond in cm.cores(split):
            guarded(cond)(lambda: f(co))

    def full(q, co):
        return view(q, co, 0, rows)

    def out(zo, co):
        q = chip(zo, 0)
        cm.send(full(q, co), s_all, rp + zo, cm.y_dev(1))
        cm.send(full(q, co), s_all, rm + zo, cm.y_dev(3))
        cm.send(full(q, co), s_core, rc + 4 * zo, cm.core_dev())

    def start(co):
        cm.send(full(cm.q, co), s_all, rz, cm.zh_dev())
        out(0, co)

    def ring(zo, co):
        q = chip(zo, -1)
        cm.recv(full(q, co), rp + zo)
        cm.send(view(q, co, 0, half), s_all, rh + zo, cm.y_dev(1))
        cm.send(full(q, co), s_core, rc + 4 * zo + 1, cm.core_dev())
        q = chip(zo, 1)
        cm.recv(full(q, co), rm + zo)
        cm.send(view(q, co, half, half), s_all, rh + zo, cm.y_dev(3))
        cm.send(full(q, co), s_core, rc + 4 * zo + 2, cm.core_dev())

    def last(zo, co):
        q = chip(zo, 2)
        cm.recv(full(q, co), rh + zo)
        cm.send(full(q, co), s_core, rc + 4 * zo + 3, cm.core_dev())

    def other_z(co):
        cm.recv(full(chip(1, 0), co), rz)
        out(1, co)

    def other_core(co):
        for zo in (0, 1):
            for i, yo in enumerate((0, -1, 1, 2)):
                cm.recv(full(chip(zo, yo), 1 - co), rc + 4 * zo + i)

    each(start)
    yield 0
    each(lambda co: ring(0, co))
    yield 1
    each(other_z)
    each(lambda co: last(0, co))
    yield 2
    each(lambda co: ring(1, co))
    yield 3
    each(lambda co: last(1, co))
    yield 4
    each(other_core)
    for co, cond in cm.cores(split):
        cm.drain_later(span(7, co), s_all, cond)
        cm.drain_later(span(8, co), s_core, cond)
    yield 5


def kernel(acts_ref, og_hbm, m_hbm, w_hbm, mnew_ref, upd_ref, wnew_ref,
           actb, ogb, rb, pb, rcb, csb, ryb, rzb, gb, hb, sb, acc1, acc2, gsq, mv, wv, ss1, ss2,
           sems, lsem):
    cm = Comm(sems)
    r, c, q = cm.r, cm.c, cm.q
    tr, tc = mnew_ref.shape
    tt = og_hbm.shape[0]

    load_o = pltpu.make_async_copy(og_hbm, ogb.at[ds(r * tt, tt, tt)], lsem.at[2])
    load_a = pltpu.make_async_copy(acts_ref, actb.at[:, ds(c * tt, tt, tt)], lsem.at[3])
    load_m = pltpu.make_async_copy(m_hbm, mv, lsem.at[0])
    load_w = pltpu.make_async_copy(w_hbm, wv, lsem.at[1])
    load_o.start()
    load_a.start()
    load_m.start()
    load_w.start()

    barrier = pltpu.get_barrier_semaphore()
    for i in range(1, 16):
        pl.semaphore_signal(barrier, inc=1, device_id=((r + i) % 16, c), device_id_type=MESH)
        pl.semaphore_signal(barrier, inc=1, device_id=(r, (c + i) % 16), device_id_type=MESH)
    load_o.wait()
    load_a.wait()
    pl.semaphore_wait(barrier, 30)

    gr = row_gather(
        cm, lambda k, lo, n, co: ogb.at[ds(k * tt + lo, n, 16)], lambda n, co: ogb.at[pl.ds(0, n)],
        tt * 3 // 4, tt // 4,
    )
    gc = col_gather(
        cm, lambda p, co, lo, n: actb.at[pl.ds(lo, n), ds((p * 2 + co) * tt, tt, tt)],
        lambda n, co: actb.at[:, pl.ds(0, n * tt)], tr,
    )
    next(gr)
    next(gc)
    for event in gr:
        if event in ((0, 0), (-1, 0), (0, 1), (-1, 1)):
            next(gc)
    for _ in gc:
        pass
    acc1[...] = jnp.zeros_like(acc1)

    @pl.loop(0, 2048 // 256)
    def _(t):
        acc1[...] += dot_nn(actb[:, ds(t * 256, 256, 256)], ogb[ds(t * 256, 256, 256), :])

    load_m.wait()
    gradient = acc1[...]
    m_new = 0.95 * mv[...] + gradient
    mnew_ref[...] = m_new
    rb[ds(r * tr, tr, tr), :] = (gradient + 0.95 * m_new).astype(BF16)

    rc1, sc1 = cm.sem(8), cm.sem()
    rcy, scy = cm.sem(2), cm.sem()
    rzx, szx = cm.sem(), cm.sem()

    def cols(ref, p, co):
        return ref.at[:, ds(p * PAIR + co * WIDE[0], WIDE[co], 128)]

    def wide(ref, co):
        return ref.at[:, pl.ds(0, WIDE[co])]

    def core_send(p):
        for co, cond in cm.cores(True):
            @pl.when(cond)
            def _():
                cm.copy(cols(pb, p, 1 - co), wide(rcb.at[p], 1 - co), sc1, rc1 + p, cm.core_dev()).start()

    def core_done(p):
        zh, y = p // 4, p % 4
        slot = (cm.y + 3 - y + 4) % 4
        for co, cond in cm.cores(True):
            @pl.when(cond)
            def _():
                cm.recv(wide(rcb.at[p], co), rc1 + p)
                mine = cols(pb, p, co)[...].astype(F32) + wide(rcb.at[p], co)[...].astype(F32)
                wide(csb.at[p], co)[...] = mine.astype(BF16)

                @pl.when(y != cm.y)
                def _():
                    cm.copy(wide(csb.at[p], co), wide(ryb.at[zh * 3 + slot % 3], co), scy, rcy + zh,
                            (r, cm.zh * 8 + y * 2 + cm.co)).start()

    def gram_pair(p):
        pb[:, ds(p * PAIR, PAIR, 128)] = dot_nt(
            rb[ds(r * tr, tr, tr), :], rb[ds(p * PAIR, PAIR, 128), :]
        ).astype(BF16)

    gr = row_gather(
        cm, lambda k, lo, n, co: rb.at[ds(k * tr + lo, n, 16)], lambda n, co: rb.at[pl.ds(0, n)],
        256, 64,
    )
    next(gr)
    last = None
    for event in gr:
        p = cm.row_pair(*event)
        gram_pair(p)
        core_send(p)
        if last is not None:
            core_done(last)
        last = p
    core_done(last)

    def y_sum(zh, co):
        for i in range(3):
            pass
        cm.recv(ryb.at[ds(zh * 3, 3, 1), :, pl.ds(0, WIDE[co])], rcy + zh)
        return (wide(csb.at[zh * 4 + cm.y], co)[...].astype(F32)
                + wide(ryb.at[zh * 3], co)[...].astype(F32)
                + wide(ryb.at[zh * 3 + 1], co)[...].astype(F32)
                + wide(ryb.at[zh * 3 + 2], co)[...].astype(F32))

    for co, cond in cm.cores(True):
        @pl.when(cond)
        def _():
            far_sum = wide(rcb.at[0], co)
            far_sum[...] = y_sum(1 - cm.zh, co).astype(BF16)
            cm.copy(far_sum, wide(rzb, co), szx, rzx, cm.zh_dev()).start()
            near_sum = y_sum(cm.zh, co)
            cm.recv(wide(rzb, co), rzx)
            tile = (near_sum + wide(rzb, co)[...].astype(F32)).astype(BF16)
            cols(gb, q, co)[...] = tile
            hb[ds(r * tr, tr, tr), pl.ds(0, WIDE[co])] = tile

    for co, cond in cm.cores(True):
        cm.drain_later(pb.at[:, pl.ds(0, 8 * WIDE[1 - co])], sc1, cond)
        cm.drain_later(pb.at[:, pl.ds(0, 6 * WIDE[co])], scy, cond)
        cm.drain_later(wide(rzb, co), szx, cond)

    def panel(ref):
        return (lambda p, co, lo, n: ref.at[pl.ds(lo, n), ds(p * PAIR + co * WIDE[0], WIDE[co], 128)],
                lambda n, co: ref.at[:, pl.ds(0, n * WIDE[co])], tr, True)

    gc = col_gather(cm, *panel(gb))
    gr = row_gather(
        cm, lambda k, lo, n, co: hb.at[ds(k * tr + lo, n, 16), pl.ds(0, WIDE[co])],
        lambda n, co: hb.at[pl.ds(0, n), pl.ds(0, WIDE[co])], 256, 64, True,
    )
    next(gr)
    next(gc)
    gsq[...] = jnp.zeros_like(gsq)

    def square(p):
        g = gb[:, ds(p * PAIR, PAIR, 128)]
        gsq[:, 0:256] += dot_nn(g, hb[ds(p * PAIR, PAIR, 128), 0:256])

        @pl.when(cm.co == 0)
        def _():
            gsq[:, 256:384] += dot_nn(g, hb[ds(p * PAIR, PAIR, 128), 256:384])

    for event in gr:
        if event in ((0, 0), (-1, 0), (0, 1)):
            next(gc)
        if event == (-1, 1):
            for _ in gc:
                pass

            @pl.loop(0, 6)
            def _(i):
                xo = i // 2 + i // 4
                square(((cm.x + xo) % 4) * 2 + i % 2)
        if event[0] == 2:
            square(cm.row_pair(*event))

    for co, cond in cm.cores(True):
        @pl.when(cond)
        def _():
            cols(sb, q, co)[...] = gsq[:, 0:WIDE[co]].astype(BF16)

    gc = col_gather(cm, *panel(sb))
    next(gc)
    squares = jnp.sum(gsq[...] * gsq[...], axis=0, keepdims=True)
    ss1[r] = jnp.broadcast_to(jnp.sum(squares, axis=1, keepdims=True), ss1.shape[1:])
    r1, s1, r2, s2 = cm.sem(), cm.sem(), cm.sem(), cm.sem()
    for i in range(1, 16):
        cm.send(ss1.at[r], s1, r1, ((r + i) % 16, c))
    acc1[...] = jnp.zeros_like(acc1)
    acc2[...] = jnp.zeros_like(acc2)

    def gram_times(lo, hi):
        @pl.loop(lo, hi)
        def _(p):
            acc1[...] += dot_nn(gb[:, ds(p * PAIR, PAIR, 128)], rb[ds(p * PAIR, PAIR, 128), :])

    def square_times():
        @pl.loop(0, 8)
        def _(p):
            acc2[...] += dot_nn(sb[:, ds(p * PAIR, PAIR, 128)], rb[ds(p * PAIR, PAIR, 128), :])

    gram_times(0, 3)
    cm.recv(ss1.at[pl.ds(0, 15)], r1)
    ss2[c] = jnp.sum(ss1[...], axis=0)
    for i in range(1, 16):
        cm.send(ss2.at[c], s2, r2, (r, (c + i) % 16))
    cm.drain_later(ss1.at[pl.ds(0, 15)], s1)
    cm.drain_later(ss2.at[pl.ds(0, 15)], s2)
    next(gc)
    gram_times(3, 5)
    next(gc)
    gram_times(5, 8)
    for _ in gc:
        pass
    square_times()
    cm.recv(ss2.at[pl.ds(0, 15)], r2)
    total = jnp.sum(ss2[...], axis=0)[0:1, 0:1]
    schatten = jnp.sqrt(total + 1e-06)
    square_root = jnp.sqrt(schatten)
    fourth_root = jnp.sqrt(square_root)
    load_w.wait()
    product = -4.775 * acc1[...] / square_root + 2.0315 * acc2[...] / schatten
    orthogonal = (3.4445 * rb[ds(r * tr, tr, tr), :].astype(F32) + product) / fourth_root
    factor = math.sqrt(D)
    upd_ref[...] = (factor * orthogonal).astype(BF16)
    wnew_ref[...] = 0.998 * wv[...] - 0.02 * factor * orthogonal
    cm.drain()


def body(acts, out_grads, momentum, weight):
    tr, tc = momentum.shape
    tt = out_grads.shape[0]
    vmem = pl.BlockSpec(memory_space=pltpu.VMEM)
    hbm = pl.BlockSpec(memory_space=pl.ANY)
    block = (tr, WIDE[0])
    return pl.pallas_call(
        kernel,
        name="muon_step",
        out_shape=(
            jax.ShapeDtypeStruct((tr, tc), F32),
            jax.ShapeDtypeStruct((tr, tc), BF16),
            jax.ShapeDtypeStruct((tr, tc), F32),
        ),
        in_specs=[hbm, hbm, hbm, hbm],
        out_specs=[vmem, vmem, vmem],
        scratch_shapes=[
            pltpu.VMEM((tr, 16 * tt), BF16),
            pltpu.VMEM((16 * tt, tc), BF16),
            pltpu.VMEM((16 * tr, tc), BF16),
            pltpu.VMEM((tr, 16 * tr), BF16),
            pltpu.VMEM((8,) + block, BF16),
            pltpu.VMEM((8,) + block, BF16),
            pltpu.VMEM((6,) + block, BF16),
            pltpu.VMEM(block, BF16),
            pltpu.VMEM((tr, 16 * tr), BF16),
            pltpu.VMEM((16 * tr, WIDE[0]), BF16),
            pltpu.VMEM((tr, 16 * tr), BF16),
            pltpu.VMEM((tr, tc), F32),
            pltpu.VMEM((tr, tc), F32),
            pltpu.VMEM(block, F32),
            pltpu.VMEM((tr, tc), F32),
            pltpu.VMEM((tr, tc), F32),
            pltpu.VMEM((16, 8, 128), F32),
            pltpu.VMEM((16, 8, 128), F32),
            pltpu.SemaphoreType.DMA((N_SEM,)),
            pltpu.SemaphoreType.DMA((4,)),
        ],
        compiler_params=pltpu.CompilerParams(
            collective_id=0, has_side_effects=True, vmem_limit_bytes=67043328
        ),
    )(acts.T, out_grads, momentum, weight)


def solution(mesh):
    in_specs = (P("col", "row"), P("row", "col"), P("row", "col"), P("row", "col"))
    out_specs = (P("row", "col"), P("row", "col"), P("row", "col"))
    return jax.shard_map(body, mesh=mesh, in_specs=in_specs, out_specs=out_specs, check_vma=False)
```
